128 devices in a mesh: dp: 16 (over y, x), expert: 4 (over z), tensor: 2 (over core).
Axes of the slice: x: 4, y: 4, z: 4, core: 2. Of those that a mesh axis runs over, the one named last changes fastest.
Arguments:
- tokens: bfloat16 [8192, 2048], P(('dp', 'expert')), may hold values from -6 to 6
- expert_ids: int32 [8192, 2], P(('dp', 'expert')), may hold values from 0 to 3, all different within a row; in each aligned block of 128 rows (0 to 127, 128 to 255, ...) at most 96 rows name the same one
- gate_values: float32 [8192, 2], P(('dp', 'expert')), may hold values from 0.1 to 1
- tag_labels: int32 [8192], P(('dp', 'expert')), may hold values from 0 to 31
- w_gate: bfloat16 [4, 2048, 7168], P('expert', 'dp', 'tensor'), may hold values from -0.125 to 0.125
- w_up: bfloat16 [4, 2048, 7168], P('expert', 'dp', 'tensor'), may hold values from -0.125 to 0.125
- w_down: bfloat16 [4, 7168, 2048], P('expert', 'tensor', 'dp'), may hold values from -0.0625 to 0.0625
- adapter_in: bfloat16 [4, 16, 2048], P('expert'), may hold values from -0.125 to 0.125
- adapter_out: bfloat16 [4, 16, 7168], P('expert', None, 'tensor'), may hold values from -1.5 to 1.5
- tag_weight: bfloat16 [2048, 32], replicated, may hold values from -0.125 to 0.125
Outputs:
- layer_out: bfloat16 [8192, 2048], P(('dp', 'expert'), 'tensor')
- in_gradient: float32 [4, 16, 2048], P('expert')
- out_gradient: float32 [4, 16, 7168], P('expert', None, 'tensor')
The draws below stay inside these ranges and needn't reach their ends.
Inputs may be any that keep to these rules, and one draw needn't show every extreme that they name: `expert_ids`: each row names 2 different experts; the rows of one index of dp and expert name each expert at most 96 times, a bound that some block reaches.
All inputs are finite; a program needn't handle non-finite values.
Results may differ from the reference program's by a relative error of at most 0.017.
Values may be sent and summed in bfloat16 or wider, within the bound.
A program may use at most 128 MiB of HBM per device.

```python
import math
import jax
import jax.numpy as jnp
import numpy as np
from jax import lax

D = 2048
FF = 7168
RANK = 16
TOP = 2
TAGS = 32
TOK_DEV = 128
EXPERTS = 4
CAP = 96
TOKENS = 8192


def with_ends(values, rng, low, largest):
    longest = values.shape.index(max(values.shape))
    spots = []
    for shift in (0, 1):
        where = [jax.random.randint(jax.random.fold_in(rng, axis), (), 0, length) for axis, length in enumerate(values.shape)]
        where[longest] = (where[longest] + shift) % values.shape[longest]
        spots.append(tuple(where))
    return values.at[spots[0]].set(low).at[spots[1]].set(largest)


def block_scale(key, extent, cuts, smallest, high):
    level = 1.0
    for axis_at, blocks in cuts:
        draws = jax.random.uniform(jax.random.fold_in(jax.random.fold_in(key, 6), axis_at), (blocks,), jnp.float32, smallest / len(cuts), high / len(cuts))
        level = level * jnp.repeat(jnp.exp(draws), extent[axis_at] // blocks).reshape((-1,) + (1,) * (len(extent) - 1 - axis_at))
    return level


def assign_block(rng, own, number, rows, count, top, limit, lean):
    sequence = jax.random.permutation(rng, count)
    heavy_load, ordinary = portions_of(count, rows * top, limit, lean, True), portions_of(count, rows * top, limit, lean, False)
    places = jnp.arange(count)

    def named(sizes, offset_by):
        used = int((sizes > 0).sum())
        fixed = max(1, used // 4)
        passed = fixed + (places - fixed + offset_by * (used - fixed)) % max(1, count - fixed)
        return jnp.zeros((count,), jnp.int32).at[sequence[jnp.where(places < fixed, places, passed)]].set(jnp.asarray(sizes, jnp.int32))

    sizes = jnp.where(number % 4 == 0, named(heavy_load, number // 4), named(ordinary, number - number // 4 - 1))
    mixed = jax.random.permutation(jax.random.fold_in(own, 3), count)
    giver, taker = mixed[0:count // 2 * 2:2], mixed[1:count // 2 * 2:2]
    margin = jnp.minimum(sizes[giver] - 1, limit - sizes[taker]) // 2
    margin = jnp.where((giver == sequence[0]) | (taker == sequence[0]) | (sizes[taker] == 0), 0, jnp.maximum(margin, 0))
    passed = jax.random.randint(jax.random.fold_in(own, 4), (count // 2,), 0, 1 << 20) % (margin + 1)
    sizes = sizes.at[giver].add(-passed).at[taker].add(passed)
    items = jnp.searchsorted(jnp.cumsum(sizes), jnp.arange(rows * top), side="right").astype(jnp.int32)
    grid = items.reshape(top, rows).T
    grid = grid[jax.random.permutation(jax.random.fold_in(own, 1), rows)]
    offset_by = jax.random.randint(jax.random.fold_in(own, 2), (rows, 1), 0, top)
    return jnp.take_along_axis(grid, (jnp.arange(top)[None, :] + offset_by) % top, axis=1)


def portions_of(count, total, limit, slope, full):
    loads = [(1 << 20) // math.isqrt(grade ** slope) + 1 for grade in range(1, count + 1)]
    largest = limit if full else min(limit, max(-(-total // count), total * loads[0] // sum(loads)))
    least = 1 if total - largest >= count - 1 else 0
    counts, rest = [largest] + [least] * (count - 1), total - largest - least * (count - 1)
    while rest > 0:
        free = [i for i in range(1, count) if counts[i] < largest] or [i for i in range(1, count) if counts[i] < limit]
        pool, remaining = sum([loads[i] for i in free]), rest
        for i in free:
            addition = min(limit - counts[i], max(1, remaining * loads[i] // pool), rest)
            counts[i] = counts[i] + addition
            rest = rest - addition
    return np.array(counts)


def centred(stream_key, shape, spread, reach, cuts=(), kind=jnp.bfloat16):
    level = block_scale(stream_key, shape, cuts, -0.22, 0.18) if cuts else 1.0
    entries = jax.random.normal(stream_key, shape, jnp.float32) * spread * level
    return jnp.minimum(jnp.maximum(entries, -reach), reach).astype(kind)


def setup_inputs(seed: int = 0) -> dict:
    key_list = jax.random.split(jax.random.key(seed), 11)
    tokens = centred(key_list[0], (TOKENS, D), 1.0, 6.0, ((0, 64),))
    expert_ids_keys = jax.random.split(jax.random.fold_in(key_list[1], 1), TOKENS // TOK_DEV)
    expert_ids_turns = jax.random.permutation(jax.random.fold_in(key_list[1], 3), TOKENS // TOK_DEV)
    expert_ids = jax.vmap(lambda own, number: assign_block(jax.random.fold_in(key_list[1], 2), own, number, TOK_DEV, EXPERTS, TOP, CAP, 2))(expert_ids_keys, expert_ids_turns).reshape((TOKENS, TOP))
    gate_values = jnp.clip(0.1 + 0.9 * jax.random.uniform(key_list[2], (TOKENS, TOP), jnp.float32) ** block_scale(key_list[2], (TOKENS, TOP), ((0, 64),), -0.2, 0.2), 0.1, 1.0)
    tag_labels = with_ends(jax.random.randint(key_list[3], (TOKENS,), 0, TAGS), jax.random.fold_in(key_list[3], 1), 0, TAGS - 1).astype(jnp.int32)
    w_gate = centred(key_list[4], (EXPERTS, D, FF), D ** -0.5, 0.125, ((0, 4), (1, 16), (2, 2)))
    w_up = centred(key_list[5], (EXPERTS, D, FF), D ** -0.5, 0.125, ((0, 4), (1, 16), (2, 2)))
    w_down = centred(key_list[6], (EXPERTS, FF, D), FF ** -0.5, 0.0625, ((0, 4), (1, 2), (2, 16)))
    adapter_in = centred(key_list[7], (EXPERTS, RANK, D), D ** -0.5, 0.125, ((0, 4),))
    adapter_out = centred(key_list[8], (EXPERTS, RANK, FF), RANK ** -0.5, 1.5, ((0, 4), (2, 2)))
    tag_weight = centred(key_list[9], (D, TAGS), D ** -0.5, 0.125)
    return {"tokens": tokens, "expert_ids": expert_ids, "gate_values": gate_values, "tag_labels": tag_labels, "w_gate": w_gate, "w_up": w_up, "w_down": w_down, "adapter_in": adapter_in, "adapter_out": adapter_out, "tag_weight": tag_weight}


adapter_scale = 2.0


def reference(tokens, expert_ids, gate_values, tag_labels, w_gate, w_up, w_down, adapter_in, adapter_out, tag_weight):
    rows_limit = (TOKENS // TOK_DEV) * CAP
    combined = tokens.astype(jnp.float32)
    stored = []
    for expert in range(EXPERTS):
        chosen = expert_ids == expert
        weight_token = jnp.sum(jnp.where(chosen, gate_values, jnp.float32(0.0)), axis=1)
        member = jnp.any(chosen, axis=1)
        picked = jnp.nonzero(member, size=rows_limit, fill_value=0)[0].astype(jnp.int32)
        valid_row = jnp.arange(rows_limit, dtype=jnp.int32) < jnp.sum(member.astype(jnp.int32))
        row_values = jnp.where(valid_row[:, None], tokens[picked], jnp.zeros((), jnp.bfloat16))
        row_weights = jnp.where(valid_row, weight_token[picked], jnp.float32(0.0))
        gate_acc = jnp.dot(row_values, w_gate[expert], preferred_element_type=jnp.float32)
        low_rank = jnp.dot(row_values, adapter_in[expert].T, preferred_element_type=jnp.float32).astype(jnp.bfloat16)
        up_full = jnp.dot(row_values, w_up[expert], preferred_element_type=jnp.float32) + adapter_scale * jnp.dot(low_rank, adapter_out[expert], preferred_element_type=jnp.float32)
        activated = jax.nn.silu(gate_acc)
        hidden = (activated * up_full).astype(jnp.bfloat16)
        result = jnp.dot(hidden, w_down[expert], preferred_element_type=jnp.float32).astype(jnp.bfloat16)
        combined = combined.at[picked].add(row_weights[:, None] * result.astype(jnp.float32))
        stored.append((picked, row_weights, row_values, low_rank, activated))
    layer_out = combined.astype(jnp.bfloat16)
    logits = jnp.dot(layer_out, tag_weight, preferred_element_type=jnp.float32)
    exp_logits = jnp.exp(logits)
    probability = exp_logits / jnp.sum(exp_logits, axis=1, keepdims=True)
    labels_hot = (tag_labels[:, None] == jnp.arange(TAGS, dtype=jnp.int32)[None, :]).astype(jnp.float32)
    logit_grad = probability - labels_hot
    upstream = jnp.dot(logit_grad, tag_weight.astype(jnp.float32).T, precision=lax.Precision.HIGHEST)
    in_list = []
    out_list = []
    for expert in range(EXPERTS):
        picked, row_weights, row_values, low_rank, activated = stored[expert]
        slot_grad = (row_weights[:, None] * upstream[picked]).astype(jnp.bfloat16)
        hidden_grad = jnp.dot(slot_grad, w_down[expert].T, preferred_element_type=jnp.float32)
        up_grad = (hidden_grad * activated).astype(jnp.bfloat16)
        out_list.append(adapter_scale * jnp.dot(low_rank.T, up_grad, preferred_element_type=jnp.float32))
        low_grad = adapter_scale * jnp.dot(up_grad, adapter_out[expert].T, preferred_element_type=jnp.float32)
        in_list.append(jnp.dot(low_grad.T, row_values.astype(jnp.float32), precision=lax.Precision.HIGHEST))
    return layer_out, jnp.stack(in_list), jnp.stack(out_list)
```

```python
import jax
import jax.numpy as jnp
from jax import lax
from jax.experimental import pallas as pl
from jax.experimental.pallas import tpu as pltpu
from jax.sharding import PartitionSpec as P

MESH = pl.DeviceIdType.MESH
BF = jnp.bfloat16
F32 = jnp.float32
EXACT = lax.Precision.HIGHEST

SIDE = 4
DIM = 2048
HALF = 1024
LANE = 128
SHARD = 3584
FQ = 896
RANK = 16
TAGS = 32
TOK = 128
CAP = 96
BLOCK = SIDE * CAP
ROWS = SIDE * BLOCK
TILE = 512


def nn(a, b):
    return lax.dot_general(a, b, (((1,), (0,)), ((), ())), preferred_element_type=F32)


def nt(a, b):
    return lax.dot_general(a, b, (((1,), (1,)), ((), ())), preferred_element_type=F32)


def tn(a, b):
    return lax.dot_general(a, b, (((0,), (0,)), ((), ())), preferred_element_type=F32)


def split(v):
    high = v.astype(BF)
    return high, (v - high.astype(F32)).astype(BF)


def kernel(
    ids_ref, gates_ref, labels_ref, tok_ref, ain_ref, aout_ref, tag_ref, wg_hbm, wu_hbm, wd_hbm,
    layer_ref, ing_ref, outg_ref,
    wg, wu, wd, tsend, xs, act, hid, low, dmat, cmat, own, oth, prt, rss, rsr, zs, ret,
    lgs, lgr, tag4, mp, gs, gx, ingp, fp, fx, ox, fy, oy, done, sem,
):
    me = lax.axis_index("dp")
    y = me // SIDE
    x = lax.rem(me, SIDE)
    z = lax.axis_index("expert")
    c = lax.axis_index("tensor")

    def at(v, d):
        return lax.rem(v + d + SIDE, SIDE)

    def dev(dx=0, dy=0, dz=0, dc=0):
        return (
            at(y, dy) * SIDE + at(x, dx),
            at(z, dz),
            lax.rem(c + dc, 2),
        )

    taken = [0]
    sent = []

    def send(src, dst, to):
        k = taken[0]
        taken[0] += 2
        copy = pltpu.make_async_remote_copy(
            src_ref=src, dst_ref=dst, send_sem=sem.at[k], recv_sem=sem.at[k + 1],
            device_id=to, device_id_type=MESH,
        )
        copy.start()
        sent.append(copy)
        return copy

    barrier = pltpu.get_barrier_semaphore()
    peers = [dev(dc=1)]
    for d in range(1, SIDE):
        peers += [dev(dx=d), dev(dy=d), dev(dz=d)]
    for peer in peers:
        pl.semaphore_signal(barrier, inc=1, device_id=peer, device_id_type=MESH)
    pl.semaphore_wait(barrier, len(peers))

    bufs = (wg, wu, wd)

    def piece(w, q):
        start = pl.multiple_of(q * FQ, LANE)
        if w == 2:
            return wd_hbm.at[0, pl.ds(start, FQ), :]
        return (wg_hbm, wu_hbm)[w].at[0, :, pl.ds(start, FQ)]

    locals_ = []
    first = [[None] * SIDE for _ in range(3)]
    ring = [[[None, None] for _ in range(SIDE)] for _ in range(3)]
    relay = [[None] * SIDE for _ in range(3)]

    def spread_y(w):
        k = taken[0]
        taken[0] += 1
        mine = pltpu.make_async_copy(piece(w, y), bufs[w].at[y, x], sem.at[k])
        mine.start()
        locals_.append(mine)
        for d in range(1, SIDE):
            first[w][d] = send(piece(w, at(y, d)), bufs[w].at[y, x], dev(dy=d))

    def spread_x(w, d):
        yy = at(y, -d)
        if d == 0:
            src = piece(w, y)
        else:
            first[w][d].wait_recv()
            src = bufs[w].at[yy, x]
        for side, step in enumerate((1, -1)):
            ring[w][d][side] = send(src, bufs[w].at[yy, x], dev(dx=step))

    def pass_on(w, d):
        yy = at(y, -d)
        side, step = (0, 1) if d < 2 else (1, -1)
        ring[w][d][side].wait_recv()
        block = bufs[w].at[yy, at(x, -step)]
        relay[w][d] = send(block, block, dev(dx=step))

    spread_y(0)
    spread_x(0, 0)
    spread_y(1)
    spread_x(1, 0)
    spread_y(2)

    before = (
        lax.broadcasted_iota(jnp.int32, (TOK, TOK), 0) < lax.broadcasted_iota(jnp.int32, (TOK, TOK), 1)
    ).astype(F32).astype(BF)
    ids = ids_ref[...]
    gates = gates_ref[...]
    spot = lax.broadcasted_iota(jnp.int32, (CAP, TOK), 0)
    for e in range(SIDE):
        uses = jnp.where(ids == e, F32(1.0), F32(0.0))
        member = uses[0:1] + uses[1:2]
        weight = uses[0:1] * gates[0:1] + uses[1:2] * gates[1:2]
        place = nn(jnp.broadcast_to(member, (16, TOK)).astype(BF), before)[0:1].astype(jnp.int32)
        hit = jnp.where(spot == place, jnp.broadcast_to(member, (CAP, TOK)), F32(0.0))
        dmat[pl.ds(e * CAP, CAP), :] = hit.astype(BF)
        cmat[pl.ds(e * CAP, CAP), :] = hit * weight
    half = tok_ref[:, pl.ds(pl.multiple_of(c * HALF, HALF), HALF)]
    tsend[...] = nn(dmat[...], half).astype(BF).reshape(SIDE, CAP, HALF)

    def rows_of(block, start=0, size=BLOCK):
        return pl.ds(pl.multiple_of(block * BLOCK + start, 32), size)

    over_z = []
    for d in range(1, SIDE):
        spot_z = pl.ds(pl.multiple_of(y * BLOCK + z * CAP, 32), CAP)
        over_z.append(send(tsend.at[at(z, d)], xs.at[c, spot_z], dev(dz=d)))
    xs[c, pl.ds(pl.multiple_of(y * BLOCK + z * CAP, 32), CAP), :] = tsend[z]

    for d in range(1, SIDE):
        spread_x(0, d)
        if d == 1:
            pass_on(0, 0)
    for copy in over_z:
        copy.wait_recv()
    block = xs.at[c, rows_of(y)]
    up_y = send(block, block, dev(dy=1))
    down_y = send(block, block, dev(dy=-1))
    to_core = [send(block, block, dev(dc=1))]
    pass_on(0, 1)
    pass_on(0, 2)
    pass_on(0, 3)
    for d in range(1, SIDE):
        spread_x(1, d)
    up_y.wait_recv()
    part = xs.at[c, rows_of(at(y, -1), 0, BLOCK // 2)]
    far_a = send(part, part, dev(dy=1))
    block = xs.at[c, rows_of(at(y, -1))]
    to_core.append(send(block, block, dev(dc=1)))
    down_y.wait_recv()
    part = xs.at[c, rows_of(at(y, 1), BLOCK // 2, BLOCK // 2)]
    far_b = send(part, part, dev(dy=-1))
    block = xs.at[c, rows_of(at(y, 1))]
    to_core.append(send(block, block, dev(dc=1)))
    far_a.wait_recv()
    far_b.wait_recv()
    block = xs.at[c, rows_of(at(y, 2))]
    to_core.append(send(block, block, dev(dc=1)))
    for copy in to_core:
        copy.wait_recv()
    for d in range(SIDE):
        pass_on(1, d)
    spread_x(2, 0)
    for d in range(1, SIDE):
        spread_x(2, d)

    def tile(i):
        return pl.ds(pl.multiple_of(i * TILE, TILE), TILE)

    def product(rows, w):
        return nn(xs[0, rows, :], w[0:2].reshape(HALF, FQ)) + nn(xs[1, rows, :], w[2:4].reshape(HALF, FQ))

    def whole(w):
        for d in range(SIDE):
            for side in range(2):
                if (d < 2) != (side == 0):
                    ring[w][d][side].wait_recv()
        for d in range(SIDE):
            relay[w][d].wait_recv()

    @pl.loop(0, ROWS // TILE)
    def _(i):
        rows = tile(i)
        low[rows, :] = (nt(xs[0, rows, :], ain_ref[:, :HALF]) + nt(xs[1, rows, :], ain_ref[:, HALF:])).astype(BF)

    locals_[0].wait()
    whole(0)

    @pl.loop(0, ROWS // TILE)
    def _(i):
        rows = tile(i)
        gate = product(rows, wg)
        act[rows, :] = gate / (1.0 + jnp.exp(-gate))

    aout = aout_ref[:, pl.ds(pl.multiple_of(y * FQ, LANE), FQ)]
    pass_on(2, 0)
    locals_[1].wait()
    whole(1)

    @pl.loop(0, ROWS // TILE)
    def _(i):
        rows = tile(i)
        up = product(rows, wu) + 2.0 * nn(low[rows, :], aout)
        hid[rows, :] = (act[rows, :] * up).astype(BF)

    pass_on(2, 1)

    to_other = [None] * SIDE
    partial = [[None] * SIDE for _ in range(SIDE)]

    def down(g, xx):
        @pl.loop(0, ROWS // TILE)
        def _(i):
            rows = tile(i)
            h = hid[rows, :]
            own[xx, rows, :] = nn(h, jnp.concatenate([wd[2 * c, xx], wd[2 * c + 1, xx]], axis=1))
            o = 1 - c
            oth[xx, rows, :] = nn(h, jnp.concatenate([wd[2 * o, xx], wd[2 * o + 1, xx]], axis=1)).astype(BF)

        to_other[g] = send(oth.at[xx], prt.at[xx], dev(dc=1))

    def scatter(g, xx):
        to_other[g].wait_recv()
        for d in range(SIDE):
            rows = rows_of(at(y, d))
            total = own[xx, rows, :] + prt[xx, rows, :].astype(F32)
            if d == 0:
                own[xx, rows, :] = total
            else:
                rss[xx, rows, :] = total.astype(BF)
                partial[g][d] = send(rss.at[xx, rows], rsr.at[d - 1, xx], dev(dy=d))

    back = []

    def give_back(g, xx):
        total = own[xx, rows_of(y), :]
        for d in range(1, SIDE):
            partial[g][d].wait_recv()
            total = total + rsr[d - 1, xx].astype(F32)
        zs[xx] = total.astype(BF).reshape(SIDE, CAP, 2 * LANE)
        mine = pl.ds(pl.multiple_of(z * CAP, 32), CAP)
        for d in range(1, SIDE):
            back.append(send(zs.at[xx, at(z, d)], ret.at[xx, mine], dev(dz=d)))
        ret[xx, mine, :] = zs[xx, z]

    groups = [x, at(x, -1), at(x, 1), at(x, 2)]
    locals_[2].wait()
    down(0, groups[0])
    pass_on(2, 2)
    pass_on(2, 3)
    ring[2][2][0].wait_recv()
    ring[2][3][0].wait_recv()
    down(1, groups[1])
    scatter(0, groups[0])
    ring[2][0][1].wait_recv()
    ring[2][1][1].wait_recv()
    down(2, groups[2])
    scatter(1, groups[1])
    for d in range(SIDE):
        relay[2][d].wait_recv()
    down(3, groups[3])
    scatter(2, groups[2])
    scatter(3, groups[3])

    copies = (
        lax.rem(lax.broadcasted_iota(jnp.int32, (TAGS, LANE), 1), TAGS)
        == lax.broadcasted_iota(jnp.int32, (TAGS, LANE), 0)
    ).astype(F32).astype(BF)
    tag4[...] = nn(tag_ref[...], copies).astype(BF)
    lane = lax.broadcasted_iota(jnp.int32, (1, LANE), 1)
    head = jnp.zeros((FQ, LANE), F32)
    for a in range(SIDE):
        cols = jnp.concatenate([wd[a, b] for b in range(SIDE)], axis=1)
        head = head + nn(cols, tag4[pl.ds(a * SIDE * LANE, SIDE * LANE), :])
    high, rest = split(head)
    kept = jnp.where(lane < 2 * TAGS, high.astype(F32), rest.astype(F32))
    mp[...] = jnp.where(lane < 3 * TAGS, kept, F32(0.0)).astype(BF)

    for g in range(SIDE):
        give_back(g, groups[g])
    for copy in back:
        copy.wait_recv()

    token_side = cmat[...].T
    c_high, c_rest = split(token_side)
    logits = jnp.zeros((TOK, LANE), F32)
    for b in range(SIDE):
        r = ret[b]
        mix = nn(c_high, r) + nn(c_rest, r)
        for j in range(2):
            cols = pl.ds((SIDE * j + b) * LANE, LANE)
            base = tok_ref[:, pl.ds(pl.multiple_of(c * HALF + (SIDE * j + b) * LANE, LANE), LANE)]
            out = (base.astype(F32) + mix[:, j * LANE : (j + 1) * LANE]).astype(BF)
            layer_ref[:, cols] = out
            head_rows = tag4[pl.ds(pl.multiple_of(c * HALF + (SIDE * j + b) * LANE, LANE), LANE), :]
            logits = logits + nn(out, head_rows)
    lgs[...] = logits
    swap = send(lgs, lgr, dev(dc=1))
    swap.wait_recv()
    logits = lgs[...] + lgr[...]
    grown = jnp.exp(logits)
    total = jnp.sum(jnp.where(lane < TAGS, grown, F32(0.0)), axis=1, keepdims=True)
    hot = lax.rem(lane, TAGS) == labels_ref[...]
    grad = grown / total - jnp.where(hot, F32(1.0), F32(0.0))
    grad = jnp.where(lane < 3 * TAGS, grad, F32(0.0))
    slot = lax.dot_general(
        cmat[...], grad, (((1,), (0,)), ((), ())), preferred_element_type=F32, precision=EXACT
    )
    high, rest = split(slot)
    middle = (lane >= TAGS) & (lane < 2 * TAGS)
    gs[...] = jnp.where(middle, rest.astype(F32), high.astype(F32)).astype(BF).reshape(SIDE, CAP, LANE)

    spot_z = pl.ds(pl.multiple_of(y * BLOCK + z * CAP, 32), CAP)
    grads_z = [send(gs.at[at(z, d)], gx.at[spot_z], dev(dz=d)) for d in range(1, SIDE)]
    gx[spot_z, :] = gs[z]
    for copy in grads_z:
        copy.wait_recv()
    block = gx.at[rows_of(y)]
    grads_y = [send(block, block, dev(dy=d)) for d in range(1, SIDE)]
    for copy in grads_y:
        copy.wait_recv()

    ingp[...] = jnp.zeros_like(ingp)
    ox[x] = jnp.zeros((RANK, FQ), F32)

    @pl.loop(0, ROWS // TILE)
    def _(i):
        rows = tile(i)
        grad_up = (nt(gx[rows, :], mp[...]) * act[rows, :]).astype(BF)
        ox[x] += 2.0 * tn(low[rows, :], grad_up)
        g_high, g_rest = split(2.0 * nt(grad_up, aout))
        for h in range(2):
            ingp[h] += tn(g_high, xs[h, rows, :]) + tn(g_rest, xs[h, rows, :])

    swap = send(ingp.at[1 - c], fp, dev(dc=1))
    outs_x = [send(ox.at[x], ox.at[x], dev(dx=d)) for d in range(1, SIDE)]
    swap.wait_recv()
    fx[x] = ingp[c] + fp[...]
    ins_x = [send(fx.at[x], fx.at[x], dev(dx=d)) for d in range(1, SIDE)]
    for copy in outs_x:
        copy.wait_recv()
    oy[y] = (ox[0] + ox[1]) + (ox[2] + ox[3])
    outs_y = [send(oy.at[y], oy.at[y], dev(dy=d)) for d in range(1, SIDE)]
    for copy in ins_x:
        copy.wait_recv()
    fy[y] = (fx[0] + fx[1]) + (fx[2] + fx[3])
    ins_y = [send(fy.at[y], fy.at[y], dev(dy=d)) for d in range(1, SIDE)]
    for copy in outs_y:
        copy.wait_recv()
    for a in range(SIDE):
        outg_ref[:, pl.ds(a * FQ, FQ)] = oy[a]
    for copy in ins_y:
        copy.wait_recv()
    fx_sum = (fy[0] + fy[1]) + (fy[2] + fy[3])
    done[c] = fx_sum
    swap = send(done.at[c], done.at[c], dev(dc=1))
    swap.wait_recv()
    ing_ref[:, :HALF] = done[0]
    ing_ref[:, HALF:] = done[1]
    for copy in sent:
        copy.wait_send()


def local(tokens, expert_ids, gate_values, tag_labels, w_gate, w_up, w_down, adapter_in, adapter_out, tag_weight):
    vmem = pl.BlockSpec(memory_space=pltpu.VMEM)
    hbm = pl.BlockSpec(memory_space=pl.ANY)
    layer, in_grad, out_grad = pl.pallas_call(
        kernel,
        out_shape=(
            jax.ShapeDtypeStruct((TOK, HALF), BF),
            jax.ShapeDtypeStruct((RANK, DIM), F32),
            jax.ShapeDtypeStruct((RANK, SHARD), F32),
        ),
        in_specs=[vmem] * 7 + [hbm] * 3,
        out_specs=(vmem, vmem, vmem),
        scratch_shapes=[
            pltpu.VMEM((SIDE, SIDE, LANE, FQ), BF),
            pltpu.VMEM((SIDE, SIDE, LANE, FQ), BF),
            pltpu.VMEM((SIDE, SIDE, FQ, LANE), BF),
            pltpu.VMEM((SIDE, CAP, HALF), BF),
            pltpu.VMEM((2, ROWS, HALF), BF),
            pltpu.VMEM((ROWS, FQ), F32),
            pltpu.VMEM((ROWS, FQ), BF),
            pltpu.VMEM((ROWS, RANK), BF),
            pltpu.VMEM((BLOCK, TOK), BF),
            pltpu.VMEM((BLOCK, TOK), F32),
            pltpu.VMEM((SIDE, ROWS, 2 * LANE), F32),
            pltpu.VMEM((SIDE, ROWS, 2 * LANE), BF),
            pltpu.VMEM((SIDE, ROWS, 2 * LANE), BF),
            pltpu.VMEM((SIDE, ROWS, 2 * LANE), BF),
            pltpu.VMEM((SIDE - 1, SIDE, BLOCK, 2 * LANE), BF),
            pltpu.VMEM((SIDE, SIDE, CAP, 2 * LANE), BF),
            pltpu.VMEM((SIDE, BLOCK, 2 * LANE), BF),
            pltpu.VMEM((TOK, LANE), F32),
            pltpu.VMEM((TOK, LANE), F32),
            pltpu.VMEM((DIM, LANE), BF),
            pltpu.VMEM((FQ, LANE), BF),
            pltpu.VMEM((SIDE, CAP, LANE), BF),
            pltpu.VMEM((ROWS, LANE), BF),
            pltpu.VMEM((2, RANK, HALF), F32),
            pltpu.VMEM((RANK, HALF), F32),
            pltpu.VMEM((SIDE, RANK, HALF), F32),
            pltpu.VMEM((SIDE, RANK, FQ), F32),
            pltpu.VMEM((SIDE, RANK, HALF), F32),
            pltpu.VMEM((SIDE, RANK, FQ), F32),
            pltpu.VMEM((2, RANK, HALF), F32),
            pltpu.SemaphoreType.DMA((256,)),
        ],
        compiler_params=pltpu.CompilerParams(
            collective_id=0, has_side_effects=True, vmem_limit_bytes=62 * 1024 * 1024
        ),
    )(
        expert_ids.T, gate_values.T, tag_labels.reshape(TOK, 1), tokens,
        adapter_in[0], adapter_out[0], tag_weight, w_gate, w_up, w_down,
    )
    return layer, in_grad[None], out_grad[None]


def solution(mesh):
    in_specs = (
        P(("dp", "expert"), None),
        P(("dp", "expert"), None),
        P(("dp", "expert"), None),
        P(("dp", "expert")),
        P("expert", "dp", "tensor"),
        P("expert", "dp", "tensor"),
        P("expert", "tensor", "dp"),
        P("expert", None, None),
        P("expert", None, "tensor"),
        P(),
    )
    out_specs = (
        P(("dp", "expert"), "tensor"),
        P("expert", None, None),
        P("expert", None, "tensor"),
    )
    return jax.shard_map(local, mesh=mesh, in_specs=in_specs, out_specs=out_specs, check_vma=False)
```

```python
import jax
import jax.numpy as jnp
from jax import lax
from jax.experimental import pallas as pl
from jax.experimental.pallas import tpu as pltpu
from jax.sharding import PartitionSpec as P

MESH = pl.DeviceIdType.MESH
BF = jnp.bfloat16
F32 = jnp.float32
EXACT = lax.Precision.HIGHEST

SIDE = 4
DIM = 2048
HALF = 1024
LANE = 128
SHARD = 3584
FQ = 896
RANK = 16
TAGS = 32
TOK = 128
CAP = 96
BLOCK = SIDE * CAP
MID = BLOCK // 2
ROWS = SIDE * BLOCK
TILE = 512


def nn(a, b):
    return lax.dot_general(a, b, (((1,), (0,)), ((), ())), preferred_element_type=F32)


def nt(a, b):
    return lax.dot_general(a, b, (((1,), (1,)), ((), ())), preferred_element_type=F32)


def tn(a, b):
    return lax.dot_general(a, b, (((0,), (0,)), ((), ())), preferred_element_type=F32)


def four(ref):
    return (ref[0].astype(F32) + ref[1].astype(F32)) + (ref[2].astype(F32) + ref[3].astype(F32))


def split(v):
    high = v.astype(BF)
    return high, (v - high.astype(F32)).astype(BF)


def kernel(
    ids_ref, gates_ref, labels_ref, tok_ref, ain_ref, aout_ref, tag_ref, wg_hbm, wu_hbm, wd_hbm,
    layer_ref, ing_ref, outg_ref,
    wg, wu, wd, tsend, xs, act, hid, low, dmat, cmat, own, oth, prt, rss, rsr, zs, ret,
    lgs, lgr, tag4, mp, gs, gx, ingp, fp, fx, ox, fy, oy, done, oacc, sem,
):
    me = lax.axis_index("dp")
    y = me // SIDE
    x = lax.rem(me, SIDE)
    z = lax.axis_index("expert")
    c = lax.axis_index("tensor")

    def at(v, d):
        return lax.rem(v + d + SIDE, SIDE)

    def dev(dx=0, dy=0, dz=0, dc=0):
        return (
            at(y, dy) * SIDE + at(x, dx),
            at(z, dz),
            lax.rem(c + dc, 2),
        )

    taken = [0]
    sent = []

    def send(src, dst, to):
        k = taken[0]
        taken[0] += 2
        copy = pltpu.make_async_remote_copy(
            src_ref=src, dst_ref=dst, send_sem=sem.at[k], recv_sem=sem.at[k + 1],
            device_id=to, device_id_type=MESH,
        )
        copy.start()
        sent.append(copy)
        return copy

    barrier = pltpu.get_barrier_semaphore()
    peers = [dev(dc=1)]
    for d in range(1, SIDE):
        peers += [dev(dx=d), dev(dy=d), dev(dz=d)]
    for peer in peers:
        pl.semaphore_signal(barrier, inc=1, device_id=peer, device_id_type=MESH)
    pl.semaphore_wait(barrier, len(peers))

    bufs = (wg, wu, wd)

    def piece(w, q):
        start = pl.multiple_of(q * FQ, LANE)
        if w == 2:
            return wd_hbm.at[0, pl.ds(start, FQ), :]
        return (wg_hbm, wu_hbm)[w].at[0, :, pl.ds(start, FQ)]

    locals_ = []
    first = [[None] * SIDE for _ in range(3)]
    ring = [[[None, None] for _ in range(SIDE)] for _ in range(3)]
    relay = [[None] * SIDE for _ in range(3)]

    def spread_y(w):
        k = taken[0]
        taken[0] += 1
        mine = pltpu.make_async_copy(piece(w, y), bufs[w].at[y, x], sem.at[k])
        mine.start()
        locals_.append(mine)
        for d in range(1, SIDE):
            first[w][d] = send(piece(w, at(y, d)), bufs[w].at[y, x], dev(dy=d))

    def spread_x(w, d):
        yy = at(y, -d)
        if d == 0:
            src = piece(w, y)
        else:
            first[w][d].wait_recv()
            src = bufs[w].at[yy, x]
        for side, step in enumerate((1, -1)):
            ring[w][d][side] = send(src, bufs[w].at[yy, x], dev(dx=step))

    def pass_on(w, d):
        yy = at(y, -d)
        side, step = (0, 1) if d < 2 else (1, -1)
        ring[w][d][side].wait_recv()
        block = bufs[w].at[yy, at(x, -step)]
        relay[w][d] = send(block, block, dev(dx=step))

    spread_y(0)
    spread_x(0, 0)
    spread_y(1)
    spread_x(1, 0)
    spread_y(2)

    before = (
        lax.broadcasted_iota(jnp.int32, (TOK, TOK), 0) < lax.broadcasted_iota(jnp.int32, (TOK, TOK), 1)
    ).astype(F32).astype(BF)
    ids = ids_ref[...]
    gates = gates_ref[...]
    spot = lax.broadcasted_iota(jnp.int32, (CAP, TOK), 0)
    for e in range(SIDE):
        uses = jnp.where(ids == e, F32(1.0), F32(0.0))
        member = uses[0:1] + uses[1:2]
        weight = uses[0:1] * gates[0:1] + uses[1:2] * gates[1:2]
        place = nn(jnp.broadcast_to(member, (16, TOK)).astype(BF), before)[0:1].astype(jnp.int32)
        hit = jnp.where(spot == place, jnp.broadcast_to(member, (CAP, TOK)), F32(0.0))
        dmat[pl.ds(e * CAP, CAP), :] = hit.astype(BF)
        cmat[pl.ds(e * CAP, CAP), :] = hit * weight
    half = tok_ref[:, pl.ds(pl.multiple_of(c * HALF, HALF), HALF)]
    tsend[...] = nn(dmat[...], half).astype(BF).reshape(SIDE, CAP, HALF)

    def rows_of(block, start=0, size=BLOCK):
        return pl.ds(pl.multiple_of(block * BLOCK + start, 32), size)

    over_z = []
    for d in range(1, SIDE):
        spot_z = pl.ds(pl.multiple_of(y * BLOCK + z * CAP, 32), CAP)
        over_z.append(send(tsend.at[at(z, d)], xs.at[c, spot_z], dev(dz=d)))
    xs[c, pl.ds(pl.multiple_of(y * BLOCK + z * CAP, 32), CAP), :] = tsend[z]

    for d in range(1, SIDE):
        spread_x(0, d)
        if d == 1:
            pass_on(0, 0)
    for copy in over_z:
        copy.wait_recv()
    block = xs.at[c, rows_of(y)]
    up_y = send(block, block, dev(dy=1))
    down_y = send(block, block, dev(dy=-1))
    to_core = [send(block, block, dev(dc=1))]
    pass_on(0, 1)
    pass_on(0, 2)
    pass_on(0, 3)
    for d in range(1, SIDE):
        spread_x(1, d)
    up_y.wait_recv()
    part = xs.at[c, rows_of(at(y, -1), 0, BLOCK // 2)]
    far_a = send(part, part, dev(dy=1))
    block = xs.at[c, rows_of(at(y, -1))]
    to_core.append(send(block, block, dev(dc=1)))
    down_y.wait_recv()
    part = xs.at[c, rows_of(at(y, 1), BLOCK // 2, BLOCK // 2)]
    far_b = send(part, part, dev(dy=-1))
    block = xs.at[c, rows_of(at(y, 1))]
    to_core.append(send(block, block, dev(dc=1)))
    far_a.wait_recv()
    far_b.wait_recv()
    block = xs.at[c, rows_of(at(y, 2))]
    to_core.append(send(block, block, dev(dc=1)))
    for copy in to_core:
        copy.wait_recv()
    for d in range(SIDE):
        pass_on(1, d)
    spread_x(2, 0)
    for d in range(1, SIDE):
        spread_x(2, d)

    def tile(i):
        return pl.ds(pl.multiple_of(i * TILE, TILE), TILE)

    def product(rows, w):
        return nn(xs[0, rows, :], w[0:2].reshape(HALF, FQ)) + nn(xs[1, rows, :], w[2:4].reshape(HALF, FQ))

    def whole(w):
        for d in range(SIDE):
            for side in range(2):
                if (d < 2) != (side == 0):
                    ring[w][d][side].wait_recv()
        for d in range(SIDE):
            relay[w][d].wait_recv()

    @pl.loop(0, ROWS // TILE)
    def _(i):
        rows = tile(i)
        low[rows, :] = (nt(xs[0, rows, :], ain_ref[:, :HALF]) + nt(xs[1, rows, :], ain_ref[:, HALF:])).astype(BF)

    locals_[0].wait()
    whole(0)

    @pl.loop(0, ROWS // TILE)
    def _(i):
        rows = tile(i)
        gate = product(rows, wg)
        act[rows, :] = gate / (1.0 + jnp.exp(-gate))

    aout = aout_ref[:, pl.ds(pl.multiple_of(y * FQ, LANE), FQ)]
    pass_on(2, 0)
    locals_[1].wait()
    whole(1)

    @pl.loop(0, ROWS // TILE)
    def _(i):
        rows = tile(i)
        up = product(rows, wu) + 2.0 * nn(low[rows, :], aout)
        hid[rows, :] = (act[rows, :] * up).astype(BF)

    pass_on(2, 1)
    pass_on(2, 2)

    to_other = [None] * SIDE
    far = [[None, None] for _ in range(SIDE)]
    near = [[] for _ in range(SIDE)]

    def down(g, xx):
        @pl.loop(0, ROWS // TILE)
        def _(i):
            rows = tile(i)
            h = hid[rows, :]
            own[xx, rows, :] = nn(h, jnp.concatenate([wd[2 * c, xx], wd[2 * c + 1, xx]], axis=1))
            o = 1 - c
            oth[xx, rows, :] = nn(h, jnp.concatenate([wd[2 * o, xx], wd[2 * o + 1, xx]], axis=1)).astype(BF)

        to_other[g] = send(oth.at[xx], prt.at[xx], dev(dc=1))

    first_half = pl.ds(0, MID)
    last_half = pl.ds(MID, MID)

    def scatter(g, xx):
        to_other[g].wait_recv()

        def total(rows):
            return own[xx, rows, :] + prt[xx, rows, :].astype(F32)

        low_rows = rows_of(at(y, 2), 0, MID)
        rss[xx, low_rows, :] = total(low_rows).astype(BF)
        far[g][0] = send(rss.at[xx, low_rows], rsr.at[1, xx, first_half], dev(dy=1))
        high_rows = rows_of(at(y, 2), MID, MID)
        rss[xx, high_rows, :] = total(high_rows).astype(BF)
        far[g][1] = send(rss.at[xx, high_rows], rsr.at[1, xx, last_half], dev(dy=-1))
        rows = rows_of(at(y, 1), MID, MID)
        rss[xx, rows, :] = total(rows).astype(BF)
        near[g].append(send(rss.at[xx, rows], rsr.at[0, xx, last_half], dev(dy=1)))
        rows = rows_of(at(y, -1), 0, MID)
        rss[xx, rows, :] = total(rows).astype(BF)
        near[g].append(send(rss.at[xx, rows], rsr.at[2, xx, first_half], dev(dy=-1)))

    def merge(g, xx):
        for side, step in enumerate((1, -1)):
            rows = rows_of(at(y, step), side * MID, MID)
            half = (first_half, last_half)[side]
            mine = own[xx, rows, :] + prt[xx, rows, :].astype(F32)
            far[g][side].wait_recv()
            rss[xx, rows, :] = (mine + rsr[1, xx, half, :].astype(F32)).astype(BF)
            near[g].append(send(rss.at[xx, rows], rsr.at[2 * side, xx, half], dev(dy=step)))

    back = []

    def give_back(g, xx):
        total = own[xx, rows_of(y), :] + prt[xx, rows_of(y), :].astype(F32)
        for copy in near[g]:
            copy.wait_recv()
        total = total + rsr[0, xx].astype(F32) + rsr[2, xx].astype(F32)
        zs[xx] = total.astype(BF).reshape(SIDE, CAP, 2 * LANE)
        mine = pl.ds(pl.multiple_of(z * CAP, 32), CAP)
        for d in range(1, SIDE):
            back.append(send(zs.at[xx, at(z, d)], ret.at[xx, mine], dev(dz=d)))
        ret[xx, mine, :] = zs[xx, z]

    groups = [x, at(x, -1), at(x, 1), at(x, 2)]
    locals_[2].wait()
    down(0, groups[0])
    pass_on(2, 3)
    ring[2][2][0].wait_recv()
    ring[2][3][0].wait_recv()
    down(1, groups[1])
    scatter(0, groups[0])
    ring[2][0][1].wait_recv()
    ring[2][1][1].wait_recv()
    down(2, groups[2])
    scatter(1, groups[1])
    merge(0, groups[0])
    for d in range(SIDE):
        relay[2][d].wait_recv()
    down(3, groups[3])
    scatter(2, groups[2])
    merge(1, groups[1])
    scatter(3, groups[3])
    merge(2, groups[2])
    give_back(0, groups[0])
    merge(3, groups[3])
    give_back(1, groups[1])

    copies = (
        lax.rem(lax.broadcasted_iota(jnp.int32, (TAGS, LANE), 1), TAGS)
        == lax.broadcasted_iota(jnp.int32, (TAGS, LANE), 0)
    ).astype(F32).astype(BF)
    tag4[...] = nn(tag_ref[...], copies).astype(BF)
    lane = lax.broadcasted_iota(jnp.int32, (1, LANE), 1)
    head = jnp.zeros((FQ, LANE), F32)
    for a in range(SIDE):
        cols = jnp.concatenate([wd[a, b] for b in range(SIDE)], axis=1)
        head = head + nn(cols, tag4[pl.ds(a * SIDE * LANE, SIDE * LANE), :])
    high, rest = split(head)
    kept = jnp.where(lane < 2 * TAGS, high.astype(F32), rest.astype(F32))
    mp[...] = jnp.where(lane < 3 * TAGS, kept, F32(0.0)).astype(BF)

    for g in range(2, SIDE):
        give_back(g, groups[g])
    for copy in back:
        copy.wait_recv()

    token_side = cmat[...].T
    c_high, c_rest = split(token_side)
    logits = jnp.zeros((TOK, LANE), F32)
    for b in range(SIDE):
        r = ret[b]
        mix = nn(c_high, r) + nn(c_rest, r)
        for j in range(2):
            cols = pl.ds((SIDE * j + b) * LANE, LANE)
            base = tok_ref[:, pl.ds(pl.multiple_of(c * HALF + (SIDE * j + b) * LANE, LANE), LANE)]
            out = (base.astype(F32) + mix[:, j * LANE : (j + 1) * LANE]).astype(BF)
            layer_ref[:, cols] = out
            head_rows = tag4[pl.ds(pl.multiple_of(c * HALF + (SIDE * j + b) * LANE, LANE), LANE), :]
            logits = logits + nn(out, head_rows)
    lgs[...] = logits
    swap = send(lgs, lgr, dev(dc=1))
    swap.wait_recv()
    logits = lgs[...] + lgr[...]
    grown = jnp.exp(logits)
    total = jnp.sum(jnp.where(lane < TAGS, grown, F32(0.0)), axis=1, keepdims=True)
    hot = lax.rem(lane, TAGS) == labels_ref[...]
    grad = grown / total - jnp.where(hot, F32(1.0), F32(0.0))
    grad = jnp.where(lane < 3 * TAGS, grad, F32(0.0))
    slot = lax.dot_general(
        cmat[...], grad, (((1,), (0,)), ((), ())), preferred_element_type=F32, precision=EXACT
    )
    high, rest = split(slot)
    middle = (lane >= TAGS) & (lane < 2 * TAGS)
    gs[...] = jnp.where(middle, rest.astype(F32), high.astype(F32)).astype(BF).reshape(SIDE, CAP, LANE)

    spot_z = pl.ds(pl.multiple_of(y * BLOCK + z * CAP, 32), CAP)
    grads_z = [send(gs.at[at(z, d)], gx.at[spot_z], dev(dz=d)) for d in range(1, SIDE)]
    gx[spot_z, :] = gs[z]
    for copy in grads_z:
        copy.wait_recv()
    block = gx.at[rows_of(y)]
    grads_y = [send(block, block, dev(dy=d)) for d in range(1, SIDE)]
    for copy in grads_y:
        copy.wait_recv()

    ingp[...] = jnp.zeros_like(ingp)
    oacc[...] = jnp.zeros_like(oacc)

    @pl.loop(0, ROWS // TILE)
    def _(i):
        rows = tile(i)
        grad_up = (nt(gx[rows, :], mp[...]) * act[rows, :]).astype(BF)
        oacc[...] += 2.0 * tn(low[rows, :], grad_up)
        low_grad = (2.0 * nt(grad_up, aout)).astype(BF)
        for h in range(2):
            ingp[h] += tn(low_grad, xs[h, rows, :])

    swap = send(ingp.at[1 - c], fp, dev(dc=1))
    ox[x] = oacc[...].astype(BF)
    outs_x = [send(ox.at[x], ox.at[x], dev(dx=d)) for d in range(1, SIDE)]
    swap.wait_recv()
    fx[x] = (ingp[c] + fp[...]).astype(BF)
    ins_x = [send(fx.at[x], fx.at[x], dev(dx=d)) for d in range(1, SIDE)]
    for copy in outs_x:
        copy.wait_recv()
    oy[y] = four(ox).astype(BF)
    outs_y = [send(oy.at[y], oy.at[y], dev(dy=d)) for d in range(1, SIDE)]
    for copy in ins_x:
        copy.wait_recv()
    fy[y] = four(fx).astype(BF)
    ins_y = [send(fy.at[y], fy.at[y], dev(dy=d)) for d in range(1, SIDE)]
    for copy in outs_y:
        copy.wait_recv()
    for a in range(SIDE):
        outg_ref[:, pl.ds(a * FQ, FQ)] = oy[a].astype(F32)
    for copy in ins_y:
        copy.wait_recv()
    done[c] = four(fy)
    swap = send(done.at[c], done.at[c], dev(dc=1))
    swap.wait_recv()
    ing_ref[:, :HALF] = done[0]
    ing_ref[:, HALF:] = done[1]
    for copy in sent:
        copy.wait_send()


def local(tokens, expert_ids, gate_values, tag_labels, w_gate, w_up, w_down, adapter_in, adapter_out, tag_weight):
    vmem = pl.BlockSpec(memory_space=pltpu.VMEM)
    hbm = pl.BlockSpec(memory_space=pl.ANY)
    layer, in_grad, out_grad = pl.pallas_call(
        kernel,
        out_shape=(
            jax.ShapeDtypeStruct((TOK, HALF), BF),
            jax.ShapeDtypeStruct((RANK, DIM), F32),
            jax.ShapeDtypeStruct((RANK, SHARD), F32),
        ),
        in_specs=[vmem] * 7 + [hbm] * 3,
        out_specs=(vmem, vmem, vmem),
        scratch_shapes=[
            pltpu.VMEM((SIDE, SIDE, LANE, FQ), BF),
            pltpu.VMEM((SIDE, SIDE, LANE, FQ), BF),
            pltpu.VMEM((SIDE, SIDE, FQ, LANE), BF),
            pltpu.VMEM((SIDE, CAP, HALF), BF),
            pltpu.VMEM((2, ROWS, HALF), BF),
            pltpu.VMEM((ROWS, FQ), F32),
            pltpu.VMEM((ROWS, FQ), BF),
            pltpu.VMEM((ROWS, RANK), BF),
            pltpu.VMEM((BLOCK, TOK), BF),
            pltpu.VMEM((BLOCK, TOK), F32),
            pltpu.VMEM((SIDE, ROWS, 2 * LANE), F32),
            pltpu.VMEM((SIDE, ROWS, 2 * LANE), BF),
            pltpu.VMEM((SIDE, ROWS, 2 * LANE), BF),
            pltpu.VMEM((SIDE, ROWS, 2 * LANE), BF),
            pltpu.VMEM((SIDE - 1, SIDE, BLOCK, 2 * LANE), BF),
            pltpu.VMEM((SIDE, SIDE, CAP, 2 * LANE), BF),
            pltpu.VMEM((SIDE, BLOCK, 2 * LANE), BF),
            pltpu.VMEM((TOK, LANE), F32),
            pltpu.VMEM((TOK, LANE), F32),
            pltpu.VMEM((DIM, LANE), BF),
            pltpu.VMEM((FQ, LANE), BF),
            pltpu.VMEM((SIDE, CAP, LANE), BF),
            pltpu.VMEM((ROWS, LANE), BF),
            pltpu.VMEM((2, RANK, HALF), F32),
            pltpu.VMEM((RANK, HALF), F32),
            pltpu.VMEM((SIDE, RANK, HALF), BF),
            pltpu.VMEM((SIDE, RANK, FQ), BF),
            pltpu.VMEM((SIDE, RANK, HALF), BF),
            pltpu.VMEM((SIDE, RANK, FQ), BF),
            pltpu.VMEM((2, RANK, HALF), F32),
            pltpu.VMEM((RANK, FQ), F32),
            pltpu.SemaphoreType.DMA((320,)),
        ],
        compiler_params=pltpu.CompilerParams(
            collective_id=0, has_side_effects=True, vmem_limit_bytes=62 * 1024 * 1024
        ),
    )(
        expert_ids.T, gate_values.T, tag_labels.reshape(TOK, 1), tokens,
        adapter_in[0], adapter_out[0], tag_weight, w_gate, w_up, w_down,
    )
    return layer, in_grad[None], out_grad[None]


def solution(mesh):
    in_specs = (
        P(("dp", "expert"), None),
        P(("dp", "expert"), None),
        P(("dp", "expert"), None),
        P(("dp", "expert")),
        P("expert", "dp", "tensor"),
        P("expert", "dp", "tensor"),
        P("expert", "tensor", "dp"),
        P("expert", None, None),
        P("expert", None, "tensor"),
        P(),
    )
    out_specs = (
        P(("dp", "expert"), "tensor"),
        P("expert", None, None),
        P("expert", None, "tensor"),
    )
    return jax.shard_map(local, mesh=mesh, in_specs=in_specs, out_specs=out_specs, check_vma=False)
```

```python
import jax
import jax.numpy as jnp
from jax import lax
from jax.experimental import pallas as pl
from jax.experimental.pallas import tpu as pltpu
from jax.sharding import PartitionSpec as P

MESH = pl.DeviceIdType.MESH
BF = jnp.bfloat16
F32 = jnp.float32
EXACT = lax.Precision.HIGHEST

SIDE = 4
DIM = 2048
HALF = 1024
LANE = 128
SHARD = 3584
FQ = 896
RANK = 16
TAGS = 32
TOK = 128
CAP = 96
BLOCK = SIDE * CAP
MID = BLOCK // 2
ROWS = SIDE * BLOCK
TILE = 512


def nn(a, b):
    return lax.dot_general(a, b, (((1,), (0,)), ((), ())), preferred_element_type=F32)


def nt(a, b):
    return lax.dot_general(a, b, (((1,), (1,)), ((), ())), preferred_element_type=F32)


def tn(a, b):
    return lax.dot_general(a, b, (((0,), (0,)), ((), ())), preferred_element_type=F32)


def four(ref):
    return (ref[0].astype(F32) + ref[1].astype(F32)) + (ref[2].astype(F32) + ref[3].astype(F32))


def split(v):
    high = v.astype(BF)
    return high, (v - high.astype(F32)).astype(BF)


def kernel(
    ids_ref, gates_ref, labels_ref, tok_ref, ain_ref, aout_ref, tag_ref, wg_hbm, wu_hbm, wd_hbm,
    layer_ref, ing_ref, outg_ref,
    wg, wu, wd, tsend, xs, act, hid, low, dmat, cmat, own, oth, prt, rss, rsr, zs, ret,
    lgs, lgr, tag4, mp, gs, gx, ingp, fp, fx, ox, fy, oy, done, oacc, sem,
):
    me = lax.axis_index("dp")
    y = me // SIDE
    x = lax.rem(me, SIDE)
    z = lax.axis_index("expert")
    c = lax.axis_index("tensor")

    def at(v, d):
        return lax.rem(v + d + SIDE, SIDE)

    def dev(dx=0, dy=0, dz=0, dc=0):
        return (
            at(y, dy) * SIDE + at(x, dx),
            at(z, dz),
            lax.rem(c + dc, 2),
        )

    taken = [0]
    sent = []

    def send(src, dst, to):
        k = taken[0]
        taken[0] += 2
        copy = pltpu.make_async_remote_copy(
            src_ref=src, dst_ref=dst, send_sem=sem.at[k], recv_sem=sem.at[k + 1],
            device_id=to, device_id_type=MESH,
        )
        copy.start()
        sent.append(copy)
        return copy

    barrier = pltpu.get_barrier_semaphore()
    peers = [dev(dc=1)]
    for d in range(1, SIDE):
        peers += [dev(dx=d), dev(dy=d), dev(dz=d)]
    for peer in peers:
        pl.semaphore_signal(barrier, inc=1, device_id=peer, device_id_type=MESH)
    pl.semaphore_wait(barrier, len(peers))

    bufs = (wg, wu, wd)

    def piece(w, q):
        start = pl.multiple_of(q * FQ, LANE)
        if w == 2:
            return wd_hbm.at[0, pl.ds(start, FQ), :]
        return (wg_hbm, wu_hbm)[w].at[0, :, pl.ds(start, FQ)]

    locals_ = []
    first = [[None] * SIDE for _ in range(3)]
    ring = [[[None, None] for _ in range(SIDE)] for _ in range(3)]
    relay = [[None] * SIDE for _ in range(3)]

    def spread_y(w):
        k = taken[0]
        taken[0] += 1
        mine = pltpu.make_async_copy(piece(w, y), bufs[w].at[y, x], sem.at[k])
        mine.start()
        locals_.append(mine)
        for d in range(1, SIDE):
            first[w][d] = send(piece(w, at(y, d)), bufs[w].at[y, x], dev(dy=d))

    def spread_x(w, d):
        yy = at(y, -d)
        if d == 0:
            src = piece(w, y)
        else:
            first[w][d].wait_recv()
            src = bufs[w].at[yy, x]
        for side, step in enumerate((1, -1)):
            ring[w][d][side] = send(src, bufs[w].at[yy, x], dev(dx=step))

    def pass_on(w, d):
        yy = at(y, -d)
        side, step = (0, 1) if d < 2 else (1, -1)
        ring[w][d][side].wait_recv()
        block = bufs[w].at[yy, at(x, -step)]
        relay[w][d] = send(block, block, dev(dx=step))

    spread_y(0)
    spread_x(0, 0)
    spread_y(1)
    spread_x(1, 0)

    before = (
        lax.broadcasted_iota(jnp.int32, (TOK, TOK), 0) < lax.broadcasted_iota(jnp.int32, (TOK, TOK), 1)
    ).astype(F32).astype(BF)
    ids = ids_ref[...]
    gates = gates_ref[...]
    spot = lax.broadcasted_iota(jnp.int32, (CAP, TOK), 0)
    for e in range(SIDE):
        uses = jnp.where(ids == e, F32(1.0), F32(0.0))
        member = uses[0:1] + uses[1:2]
        weight = uses[0:1] * gates[0:1] + uses[1:2] * gates[1:2]
        place = nn(jnp.broadcast_to(member, (16, TOK)).astype(BF), before)[0:1].astype(jnp.int32)
        hit = jnp.where(spot == place, jnp.broadcast_to(member, (CAP, TOK)), F32(0.0))
        dmat[pl.ds(e * CAP, CAP), :] = hit.astype(BF)
        cmat[pl.ds(e * CAP, CAP), :] = hit * weight
    half = tok_ref[:, pl.ds(pl.multiple_of(c * HALF, HALF), HALF)]
    tsend[...] = nn(dmat[...], half).astype(BF).reshape(SIDE, CAP, HALF)

    def rows_of(block, start=0, size=BLOCK):
        return pl.ds(pl.multiple_of(block * BLOCK + start, 32), size)

    over_z = []
    for d in range(1, SIDE):
        spot_z = pl.ds(pl.multiple_of(y * BLOCK + z * CAP, 32), CAP)
        over_z.append(send(tsend.at[at(z, d)], xs.at[c, spot_z], dev(dz=d)))
    xs[c, pl.ds(pl.multiple_of(y * BLOCK + z * CAP, 32), CAP), :] = tsend[z]

    for d in range(1, SIDE):
        spread_x(0, d)
        if d == 1:
            pass_on(0, 0)
    for copy in over_z:
        copy.wait_recv()
    block = xs.at[c, rows_of(y)]
    up_y = send(block, block, dev(dy=1))
    down_y = send(block, block, dev(dy=-1))
    to_core = [send(block, block, dev(dc=1))]
    pass_on(0, 1)
    pass_on(0, 2)
    pass_on(0, 3)
    for d in range(1, SIDE):
        spread_x(1, d)
    up_y.wait_recv()
    part = xs.at[c, rows_of(at(y, -1), 0, BLOCK // 2)]
    far_a = send(part, part, dev(dy=1))
    block = xs.at[c, rows_of(at(y, -1))]
    to_core.append(send(block, block, dev(dc=1)))
    down_y.wait_recv()
    part = xs.at[c, rows_of(at(y, 1), BLOCK // 2, BLOCK // 2)]
    far_b = send(part, part, dev(dy=-1))
    spread_y(2)
    block = xs.at[c, rows_of(at(y, 1))]
    to_core.append(send(block, block, dev(dc=1)))
    for d in range(SIDE):
        pass_on(1, d)
    spread_x(2, 0)
    far_a.wait_recv()
    far_b.wait_recv()
    block = xs.at[c, rows_of(at(y, 2))]
    to_core.append(send(block, block, dev(dc=1)))
    for copy in to_core:
        copy.wait_recv()

    def tile(i):
        return pl.ds(pl.multiple_of(i * TILE, TILE), TILE)

    def product(rows, w):
        return nn(xs[0, rows, :], w[0:2].reshape(HALF, FQ)) + nn(xs[1, rows, :], w[2:4].reshape(HALF, FQ))

    def whole(w):
        for d in range(SIDE):
            for side in range(2):
                if (d < 2) != (side == 0):
                    ring[w][d][side].wait_recv()
        for d in range(SIDE):
            relay[w][d].wait_recv()

    @pl.loop(0, ROWS // TILE)
    def _(i):
        rows = tile(i)
        low[rows, :] = (nt(xs[0, rows, :], ain_ref[:, :HALF]) + nt(xs[1, rows, :], ain_ref[:, HALF:])).astype(BF)

    locals_[0].wait()
    whole(0)

    @pl.loop(0, ROWS // TILE)
    def _(i):
        rows = tile(i)
        gate = product(rows, wg)
        act[rows, :] = gate / (1.0 + jnp.exp(-gate))

    aout = aout_ref[:, pl.ds(pl.multiple_of(y * FQ, LANE), FQ)]
    for d in range(1, SIDE):
        spread_x(2, d)
    locals_[1].wait()
    whole(1)

    @pl.loop(0, ROWS // TILE)
    def _(i):
        rows = tile(i)
        up = product(rows, wu) + 2.0 * nn(low[rows, :], aout)
        hid[rows, :] = (act[rows, :] * up).astype(BF)

    for d in range(3):
        pass_on(2, d)

    to_other = [None] * SIDE
    far = [[None, None] for _ in range(SIDE)]
    near = [[] for _ in range(SIDE)]

    def down(g, xx):
        @pl.loop(0, ROWS // TILE)
        def _(i):
            rows = tile(i)
            h = hid[rows, :]
            own[xx, rows, :] = nn(h, jnp.concatenate([wd[2 * c, xx], wd[2 * c + 1, xx]], axis=1))
            o = 1 - c
            oth[xx, rows, :] = nn(h, jnp.concatenate([wd[2 * o, xx], wd[2 * o + 1, xx]], axis=1)).astype(BF)

        to_other[g] = send(oth.at[xx], prt.at[xx], dev(dc=1))

    first_half = pl.ds(0, MID)
    last_half = pl.ds(MID, MID)

    def scatter(g, xx):
        to_other[g].wait_recv()

        def total(rows):
            return own[xx, rows, :] + prt[xx, rows, :].astype(F32)

        low_rows = rows_of(at(y, 2), 0, MID)
        rss[xx, low_rows, :] = total(low_rows).astype(BF)
        far[g][0] = send(rss.at[xx, low_rows], rsr.at[1, xx, first_half], dev(dy=1))
        high_rows = rows_of(at(y, 2), MID, MID)
        rss[xx, high_rows, :] = total(high_rows).astype(BF)
        far[g][1] = send(rss.at[xx, high_rows], rsr.at[1, xx, last_half], dev(dy=-1))
        rows = rows_of(at(y, 1), MID, MID)
        rss[xx, rows, :] = total(rows).astype(BF)
        near[g].append(send(rss.at[xx, rows], rsr.at[0, xx, last_half], dev(dy=1)))
        rows = rows_of(at(y, -1), 0, MID)
        rss[xx, rows, :] = total(rows).astype(BF)
        near[g].append(send(rss.at[xx, rows], rsr.at[2, xx, first_half], dev(dy=-1)))

    def merge(g, xx):
        for side, step in enumerate((1, -1)):
            rows = rows_of(at(y, step), side * MID, MID)
            half = (first_half, last_half)[side]
            mine = own[xx, rows, :] + prt[xx, rows, :].astype(F32)
            far[g][side].wait_recv()
            rss[xx, rows, :] = (mine + rsr[1, xx, half, :].astype(F32)).astype(BF)
            near[g].append(send(rss.at[xx, rows], rsr.at[2 * side, xx, half], dev(dy=step)))

    back = []

    def give_back(g, xx):
        total = own[xx, rows_of(y), :] + prt[xx, rows_of(y), :].astype(F32)
        for copy in near[g]:
            copy.wait_recv()
        total = total + rsr[0, xx].astype(F32) + rsr[2, xx].astype(F32)
        zs[xx] = total.astype(BF).reshape(SIDE, CAP, 2 * LANE)
        mine = pl.ds(pl.multiple_of(z * CAP, 32), CAP)
        for d in range(1, SIDE):
            back.append(send(zs.at[xx, at(z, d)], ret.at[xx, mine], dev(dz=d)))
        ret[xx, mine, :] = zs[xx, z]

    groups = [x, at(x, -1), at(x, 1), at(x, 2)]
    locals_[2].wait()
    down(0, groups[0])
    pass_on(2, 3)
    ring[2][2][0].wait_recv()
    ring[2][3][0].wait_recv()
    down(1, groups[1])
    scatter(0, groups[0])
    ring[2][0][1].wait_recv()
    ring[2][1][1].wait_recv()
    down(2, groups[2])
    scatter(1, groups[1])
    merge(0, groups[0])
    for d in range(SIDE):
        relay[2][d].wait_recv()
    down(3, groups[3])
    scatter(2, groups[2])
    merge(1, groups[1])
    scatter(3, groups[3])
    merge(2, groups[2])
    give_back(0, groups[0])
    merge(3, groups[3])
    give_back(1, groups[1])

    copies = (
        lax.rem(lax.broadcasted_iota(jnp.int32, (TAGS, LANE), 1), TAGS)
        == lax.broadcasted_iota(jnp.int32, (TAGS, LANE), 0)
    ).astype(F32).astype(BF)
    tag4[...] = nn(tag_ref[...], copies).astype(BF)
    lane = lax.broadcasted_iota(jnp.int32, (1, LANE), 1)
    head = jnp.zeros((FQ, LANE), F32)
    for a in range(SIDE):
        cols = jnp.concatenate([wd[a, b] for b in range(SIDE)], axis=1)
        head = head + nn(cols, tag4[pl.ds(a * SIDE * LANE, SIDE * LANE), :])
    high, rest = split(head)
    kept = jnp.where(lane < 2 * TAGS, high.astype(F32), rest.astype(F32))
    mp[...] = jnp.where(lane < 3 * TAGS, kept, F32(0.0)).astype(BF)

    for g in range(2, SIDE):
        give_back(g, groups[g])
    for copy in back:
        copy.wait_recv()

    token_side = cmat[...].T
    c_high, c_rest = split(token_side)
    logits = jnp.zeros((TOK, LANE), F32)
    for b in range(SIDE):
        r = ret[b]
        mix = nn(c_high, r) + nn(c_rest, r)
        for j in range(2):
            cols = pl.ds((SIDE * j + b) * LANE, LANE)
            base = tok_ref[:, pl.ds(pl.multiple_of(c * HALF + (SIDE * j + b) * LANE, LANE), LANE)]
            out = (base.astype(F32) + mix[:, j * LANE : (j + 1) * LANE]).astype(BF)
            layer_ref[:, cols] = out
            head_rows = tag4[pl.ds(pl.multiple_of(c * HALF + (SIDE * j + b) * LANE, LANE), LANE), :]
            logits = logits + nn(out, head_rows)
    lgs[...] = logits
    swap = send(lgs, lgr, dev(dc=1))
    swap.wait_recv()
    logits = lgs[...] + lgr[...]
    grown = jnp.exp(logits)
    total = jnp.sum(jnp.where(lane < TAGS, grown, F32(0.0)), axis=1, keepdims=True)
    hot = lax.rem(lane, TAGS) == labels_ref[...]
    grad = grown / total - jnp.where(hot, F32(1.0), F32(0.0))
    grad = jnp.where(lane < 3 * TAGS, grad, F32(0.0))
    slot = lax.dot_general(
        cmat[...], grad, (((1,), (0,)), ((), ())), preferred_element_type=F32, precision=EXACT
    )
    high, rest = split(slot)
    middle = (lane >= TAGS) & (lane < 2 * TAGS)
    gs[...] = jnp.where(middle, rest.astype(F32), high.astype(F32)).astype(BF).reshape(SIDE, CAP, LANE)

    spot_z = pl.ds(pl.multiple_of(y * BLOCK + z * CAP, 32), CAP)
    grads_z = [send(gs.at[at(z, d)], gx.at[spot_z], dev(dz=d)) for d in range(1, SIDE)]
    gx[spot_z, :] = gs[z]
    for copy in grads_z:
        copy.wait_recv()
    block = gx.at[rows_of(y)]
    grads_y = [send(block, block, dev(dy=d)) for d in range(1, SIDE)]
    for copy in grads_y:
        copy.wait_recv()

    ingp[...] = jnp.zeros_like(ingp)
    oacc[...] = jnp.zeros_like(oacc)

    @pl.loop(0, ROWS // TILE)
    def _(i):
        rows = tile(i)
        grad_up = (nt(gx[rows, :], mp[...]) * act[rows, :]).astype(BF)
        oacc[...] += 2.0 * tn(low[rows, :], grad_up)
        low_grad = (2.0 * nt(grad_up, aout)).astype(BF)
        for h in range(2):
            ingp[h] += tn(low_grad, xs[h, rows, :])

    swap = send(ingp.at[1 - c], fp, dev(dc=1))
    ox[x] = oacc[...].astype(BF)
    outs_x = [send(ox.at[x], ox.at[x], dev(dx=d)) for d in range(1, SIDE)]
    swap.wait_recv()
    fx[x] = (ingp[c] + fp[...]).astype(BF)
    ins_x = [send(fx.at[x], fx.at[x], dev(dx=d)) for d in range(1, SIDE)]
    for copy in outs_x:
        copy.wait_recv()
    oy[y] = four(ox).astype(BF)
    outs_y = [send(oy.at[y], oy.at[y], dev(dy=d)) for d in range(1, SIDE)]
    for copy in ins_x:
        copy.wait_recv()
    fy[y] = four(fx).astype(BF)
    ins_y = [send(fy.at[y], fy.at[y], dev(dy=d)) for d in range(1, SIDE)]
    for copy in outs_y:
        copy.wait_recv()
    for a in range(SIDE):
        outg_ref[:, pl.ds(a * FQ, FQ)] = oy[a].astype(F32)
    for copy in ins_y:
        copy.wait_recv()
    done[c] = four(fy)
    swap = send(done.at[c], done.at[c], dev(dc=1))
    swap.wait_recv()
    ing_ref[:, :HALF] = done[0]
    ing_ref[:, HALF:] = done[1]
    for copy in sent:
        copy.wait_send()


def local(tokens, expert_ids, gate_values, tag_labels, w_gate, w_up, w_down, adapter_in, adapter_out, tag_weight):
    vmem = pl.BlockSpec(memory_space=pltpu.VMEM)
    hbm = pl.BlockSpec(memory_space=pl.ANY)
    layer, in_grad, out_grad = pl.pallas_call(
        kernel,
        out_shape=(
            jax.ShapeDtypeStruct((TOK, HALF), BF),
            jax.ShapeDtypeStruct((RANK, DIM), F32),
            jax.ShapeDtypeStruct((RANK, SHARD), F32),
        ),
        in_specs=[vmem] * 7 + [hbm] * 3,
        out_specs=(vmem, vmem, vmem),
        scratch_shapes=[
            pltpu.VMEM((SIDE, SIDE, LANE, FQ), BF),
            pltpu.VMEM((SIDE, SIDE, LANE, FQ), BF),
            pltpu.VMEM((SIDE, SIDE, FQ, LANE), BF),
            pltpu.VMEM((SIDE, CAP, HALF), BF),
            pltpu.VMEM((2, ROWS, HALF), BF),
            pltpu.VMEM((ROWS, FQ), F32),
            pltpu.VMEM((ROWS, FQ), BF),
            pltpu.VMEM((ROWS, RANK), BF),
            pltpu.VMEM((BLOCK, TOK), BF),
            pltpu.VMEM((BLOCK, TOK), F32),
            pltpu.VMEM((SIDE, ROWS, 2 * LANE), F32),
            pltpu.VMEM((SIDE, ROWS, 2 * LANE), BF),
            pltpu.VMEM((SIDE, ROWS, 2 * LANE), BF),
            pltpu.VMEM((SIDE, ROWS, 2 * LANE), BF),
            pltpu.VMEM((SIDE - 1, SIDE, BLOCK, 2 * LANE), BF),
            pltpu.VMEM((SIDE, SIDE, CAP, 2 * LANE), BF),
            pltpu.VMEM((SIDE, BLOCK, 2 * LANE), BF),
            pltpu.VMEM((TOK, LANE), F32),
            pltpu.VMEM((TOK, LANE), F32),
            pltpu.VMEM((DIM, LANE), BF),
            pltpu.VMEM((FQ, LANE), BF),
            pltpu.VMEM((SIDE, CAP, LANE), BF),
            pltpu.VMEM((ROWS, LANE), BF),
            pltpu.VMEM((2, RANK, HALF), F32),
            pltpu.VMEM((RANK, HALF), F32),
            pltpu.VMEM((SIDE, RANK, HALF), BF),
            pltpu.VMEM((SIDE, RANK, FQ), BF),
            pltpu.VMEM((SIDE, RANK, HALF), BF),
            pltpu.VMEM((SIDE, RANK, FQ), BF),
            pltpu.VMEM((2, RANK, HALF), F32),
            pltpu.VMEM((RANK, FQ), F32),
            pltpu.SemaphoreType.DMA((320,)),
        ],
        compiler_params=pltpu.CompilerParams(
            collective_id=0, has_side_effects=True, vmem_limit_bytes=62 * 1024 * 1024
        ),
    )(
        expert_ids.T, gate_values.T, tag_labels.reshape(TOK, 1), tokens,
        adapter_in[0], adapter_out[0], tag_weight, w_gate, w_up, w_down,
    )
    return layer, in_grad[None], out_grad[None]


def solution(mesh):
    in_specs = (
        P(("dp", "expert"), None),
        P(("dp", "expert"), None),
        P(("dp", "expert"), None),
        P(("dp", "expert")),
        P("expert", "dp", "tensor"),
        P("expert", "dp", "tensor"),
        P("expert", "tensor", "dp"),
        P("expert", None, None),
        P("expert", None, "tensor"),
        P(),
    )
    out_specs = (
        P(("dp", "expert"), "tensor"),
        P("expert", None, None),
        P("expert", None, "tensor"),
    )
    return jax.shard_map(local, mesh=mesh, in_specs=in_specs, out_specs=out_specs, check_vma=False)
```

```python
import jax
import jax.numpy as jnp
from jax import lax
from jax.experimental import pallas as pl
from jax.experimental.pallas import tpu as pltpu
from jax.sharding import PartitionSpec as P

MESH = pl.DeviceIdType.MESH
BF = jnp.bfloat16
F32 = jnp.float32
EXACT = lax.Precision.HIGHEST

SIDE = 4
DIM = 2048
HALF = 1024
LANE = 128
SHARD = 3584
FQ = 896
RANK = 16
TAGS = 32
TOK = 128
CAP = 96
BLOCK = SIDE * CAP
MID = BLOCK // 2
ROWS = SIDE * BLOCK
TILE = 512


def nn(a, b):
    return lax.dot_general(a, b, (((1,), (0,)), ((), ())), preferred_element_type=F32)


def nt(a, b):
    return lax.dot_general(a, b, (((1,), (1,)), ((), ())), preferred_element_type=F32)


def tn(a, b):
    return lax.dot_general(a, b, (((0,), (0,)), ((), ())), preferred_element_type=F32)


def four(ref):
    return (ref[0].astype(F32) + ref[1].astype(F32)) + (ref[2].astype(F32) + ref[3].astype(F32))


def split(v):
    high = v.astype(BF)
    return high, (v - high.astype(F32)).astype(BF)


def kernel(
    ids_ref, gates_ref, labels_ref, tok_ref, ain_ref, aout_ref, tag_ref, wg_hbm, wu_hbm, wd_hbm,
    layer_ref, ing_ref, outg_ref,
    wg, wu, wd, tsend, xs, act, hid, low, dmat, cmat, own, oth, prt, rss, rsr, zs, ret,
    lgs, lgr, tag4, mp, gs, gx, ingp, fp, fx, ox, fy, oy, done, oacc, sem,
):
    me = lax.axis_index("dp")
    y = me // SIDE
    x = lax.rem(me, SIDE)
    z = lax.axis_index("expert")
    c = lax.axis_index("tensor")

    def at(v, d):
        return lax.rem(v + d + SIDE, SIDE)

    def dev(dx=0, dy=0, dz=0, dc=0):
        return (
            at(y, dy) * SIDE + at(x, dx),
            at(z, dz),
            lax.rem(c + dc, 2),
        )

    taken = [0]
    sent = []

    def send(src, dst, to):
        k = taken[0]
        taken[0] += 2
        copy = pltpu.make_async_remote_copy(
            src_ref=src, dst_ref=dst, send_sem=sem.at[k], recv_sem=sem.at[k + 1],
            device_id=to, device_id_type=MESH,
        )
        copy.start()
        sent.append(copy)
        return copy

    barrier = pltpu.get_barrier_semaphore()
    peers = [dev(dc=1)]
    for d in range(1, SIDE):
        peers += [dev(dx=d), dev(dy=d), dev(dz=d)]
    for peer in peers:
        pl.semaphore_signal(barrier, inc=1, device_id=peer, device_id_type=MESH)
    pl.semaphore_wait(barrier, len(peers))

    bufs = (wg, wu, wd)

    def piece(w, q):
        start = pl.multiple_of(q * FQ, LANE)
        if w == 2:
            return wd_hbm.at[0, pl.ds(start, FQ), :]
        return (wg_hbm, wu_hbm)[w].at[0, :, pl.ds(start, FQ)]

    locals_ = []
    first = [[None] * SIDE for _ in range(3)]
    ring = [[[None, None] for _ in range(SIDE)] for _ in range(3)]
    relay = [[None] * SIDE for _ in range(3)]

    def spread_y(w):
        k = taken[0]
        taken[0] += 1
        mine = pltpu.make_async_copy(piece(w, y), bufs[w].at[y, x], sem.at[k])
        mine.start()
        locals_.append(mine)
        for d in range(1, SIDE):
            first[w][d] = send(piece(w, at(y, d)), bufs[w].at[y, x], dev(dy=d))

    def spread_x(w, d):
        yy = at(y, -d)
        if d == 0:
            src = piece(w, y)
        else:
            first[w][d].wait_recv()
            src = bufs[w].at[yy, x]
        for side, step in enumerate((1, -1)):
            ring[w][d][side] = send(src, bufs[w].at[yy, x], dev(dx=step))

    def pass_on(w, d):
        yy = at(y, -d)
        side, step = (0, 1) if d < 2 else (1, -1)
        ring[w][d][side].wait_recv()
        block = bufs[w].at[yy, at(x, -step)]
        relay[w][d] = send(block, block, dev(dx=step))

    spread_y(0)
    spread_x(0, 0)
    spread_y(1)
    spread_x(1, 0)

    before = (
        lax.broadcasted_iota(jnp.int32, (TOK, TOK), 0) < lax.broadcasted_iota(jnp.int32, (TOK, TOK), 1)
    ).astype(F32).astype(BF)
    ids = ids_ref[...]
    gates = gates_ref[...]
    spot = lax.broadcasted_iota(jnp.int32, (CAP, TOK), 0)
    for e in range(SIDE):
        uses = jnp.where(ids == e, F32(1.0), F32(0.0))
        member = uses[0:1] + uses[1:2]
        weight = uses[0:1] * gates[0:1] + uses[1:2] * gates[1:2]
        place = nn(jnp.broadcast_to(member, (16, TOK)).astype(BF), before)[0:1].astype(jnp.int32)
        hit = jnp.where(spot == place, jnp.broadcast_to(member, (CAP, TOK)), F32(0.0))
        dmat[pl.ds(e * CAP, CAP), :] = hit.astype(BF)
        cmat[pl.ds(e * CAP, CAP), :] = hit * weight
    half = tok_ref[:, pl.ds(pl.multiple_of(c * HALF, HALF), HALF)]
    tsend[...] = nn(dmat[...], half).astype(BF).reshape(SIDE, CAP, HALF)

    def rows_of(block, start=0, size=BLOCK):
        return pl.ds(pl.multiple_of(block * BLOCK + start, 32), size)

    over_z = []
    for d in range(1, SIDE):
        spot_z = pl.ds(pl.multiple_of(y * BLOCK + z * CAP, 32), CAP)
        over_z.append(send(tsend.at[at(z, d)], xs.at[c, spot_z], dev(dz=d)))
    xs[c, pl.ds(pl.multiple_of(y * BLOCK + z * CAP, 32), CAP), :] = tsend[z]

    for d in range(1, SIDE):
        spread_x(0, d)
        if d == 1:
            pass_on(0, 0)
    for copy in over_z:
        copy.wait_recv()
    block = xs.at[c, rows_of(y)]
    up_y = send(block, block, dev(dy=1))
    down_y = send(block, block, dev(dy=-1))
    to_core = [send(block, block, dev(dc=1))]
    pass_on(0, 1)
    pass_on(0, 2)
    pass_on(0, 3)
    for d in range(1, SIDE):
        spread_x(1, d)
    up_y.wait_recv()
    part = xs.at[c, rows_of(at(y, -1), 0, BLOCK // 2)]
    far_a = send(part, part, dev(dy=1))
    block = xs.at[c, rows_of(at(y, -1))]
    to_core.append(send(block, block, dev(dc=1)))
    down_y.wait_recv()
    part = xs.at[c, rows_of(at(y, 1), BLOCK // 2, BLOCK // 2)]
    far_b = send(part, part, dev(dy=-1))
    spread_y(2)
    block = xs.at[c, rows_of(at(y, 1))]
    to_core.append(send(block, block, dev(dc=1)))
    for d in range(SIDE):
        pass_on(1, d)
    spread_x(2, 0)
    far_a.wait_recv()
    far_b.wait_recv()
    block = xs.at[c, rows_of(at(y, 2))]
    to_core.append(send(block, block, dev(dc=1)))
    for copy in to_core:
        copy.wait_recv()

    def tile(i):
        return pl.ds(pl.multiple_of(i * TILE, TILE), TILE)

    def product(rows, w):
        return nn(xs[0, rows, :], w[0:2].reshape(HALF, FQ)) + nn(xs[1, rows, :], w[2:4].reshape(HALF, FQ))

    def whole(w):
        for d in range(SIDE):
            for side in range(2):
                if (d < 2) != (side == 0):
                    ring[w][d][side].wait_recv()
        for d in range(SIDE):
            relay[w][d].wait_recv()

    @pl.loop(0, ROWS // TILE)
    def _(i):
        rows = tile(i)
        low[rows, :] = (nt(xs[0, rows, :], ain_ref[:, :HALF]) + nt(xs[1, rows, :], ain_ref[:, HALF:])).astype(BF)

    locals_[0].wait()
    whole(0)

    @pl.loop(0, ROWS // TILE)
    def _(i):
        rows = tile(i)
        gate = product(rows, wg)
        act[rows, :] = gate / (1.0 + jnp.exp(-gate))

    aout = aout_ref[:, pl.ds(pl.multiple_of(y * FQ, LANE), FQ)]
    for d in range(1, SIDE):
        spread_x(2, d)
    locals_[1].wait()
    whole(1)

    @pl.loop(0, ROWS // TILE)
    def _(i):
        rows = tile(i)
        up = product(rows, wu) + 2.0 * nn(low[rows, :], aout)
        hid[rows, :] = (act[rows, :] * up).astype(BF)

    for d in range(3):
        pass_on(2, d)

    to_other = [None] * SIDE
    far = [[None, None] for _ in range(SIDE)]
    near = [[] for _ in range(SIDE)]

    def down(g, xx):
        @pl.loop(0, ROWS // TILE)
        def _(i):
            rows = tile(i)
            h = hid[rows, :]
            own[xx, rows, :] = nn(h, jnp.concatenate([wd[2 * c, xx], wd[2 * c + 1, xx]], axis=1))
            o = 1 - c
            oth[xx, rows, :] = nn(h, jnp.concatenate([wd[2 * o, xx], wd[2 * o + 1, xx]], axis=1)).astype(BF)

        to_other[g] = send(oth.at[xx], prt.at[xx], dev(dc=1))

    first_half = pl.ds(0, MID)
    last_half = pl.ds(MID, MID)

    def scatter(g, xx):
        to_other[g].wait_recv()

        def total(rows):
            return own[xx, rows, :] + prt[xx, rows, :].astype(F32)

        low_rows = rows_of(at(y, 2), 0, MID)
        rss[xx, low_rows, :] = total(low_rows).astype(BF)
        far[g][0] = send(rss.at[xx, low_rows], rsr.at[1, xx, first_half], dev(dy=1))
        high_rows = rows_of(at(y, 2), MID, MID)
        rss[xx, high_rows, :] = total(high_rows).astype(BF)
        far[g][1] = send(rss.at[xx, high_rows], rsr.at[1, xx, last_half], dev(dy=-1))
        rows = rows_of(at(y, 1), MID, MID)
        rss[xx, rows, :] = total(rows).astype(BF)
        near[g].append(send(rss.at[xx, rows], rsr.at[0, xx, last_half], dev(dy=1)))
        rows = rows_of(at(y, -1), 0, MID)
        rss[xx, rows, :] = total(rows).astype(BF)
        near[g].append(send(rss.at[xx, rows], rsr.at[2, xx, first_half], dev(dy=-1)))

    def merge(g, xx):
        for side, step in enumerate((1, -1)):
            rows = rows_of(at(y, step), side * MID, MID)
            half = (first_half, last_half)[side]
            mine = own[xx, rows, :] + prt[xx, rows, :].astype(F32)
            far[g][side].wait_recv()
            rss[xx, rows, :] = (mine + rsr[1, xx, half, :].astype(F32)).astype(BF)
            near[g].append(send(rss.at[xx, rows], rsr.at[2 * side, xx, half], dev(dy=step)))

    back = []

    def give_back(g, xx):
        total = own[xx, rows_of(y), :] + prt[xx, rows_of(y), :].astype(F32)
        for copy in near[g]:
            copy.wait_recv()
        total = total + rsr[0, xx].astype(F32) + rsr[2, xx].astype(F32)
        zs[xx] = total.astype(BF).reshape(SIDE, CAP, 2 * LANE)
        mine = pl.ds(pl.multiple_of(z * CAP, 32), CAP)
        for d in range(1, SIDE):
            back.append(send(zs.at[xx, at(z, d)], ret.at[xx, mine], dev(dz=d)))
        ret[xx, mine, :] = zs[xx, z]

    groups = [x, at(x, -1), at(x, 1), at(x, 2)]
    locals_[2].wait()
    down(0, groups[0])
    pass_on(2, 3)
    ring[2][2][0].wait_recv()
    ring[2][3][0].wait_recv()
    down(1, groups[1])
    scatter(0, groups[0])
    ring[2][0][1].wait_recv()
    ring[2][1][1].wait_recv()
    down(2, groups[2])
    scatter(1, groups[1])
    merge(0, groups[0])
    for d in range(SIDE):
        relay[2][d].wait_recv()
    down(3, groups[3])
    scatter(2, groups[2])
    merge(1, groups[1])
    scatter(3, groups[3])
    merge(2, groups[2])
    give_back(0, groups[0])
    merge(3, groups[3])
    give_back(1, groups[1])

    copies = (
        lax.rem(lax.broadcasted_iota(jnp.int32, (TAGS, LANE), 1), TAGS)
        == lax.broadcasted_iota(jnp.int32, (TAGS, LANE), 0)
    ).astype(F32).astype(BF)
    tag4[...] = nn(tag_ref[...], copies).astype(BF)
    lane = lax.broadcasted_iota(jnp.int32, (1, LANE), 1)
    head = jnp.zeros((FQ, LANE), F32)
    for a in range(SIDE):
        cols = jnp.concatenate([wd[a, b] for b in range(SIDE)], axis=1)
        head = head + nn(cols, tag4[pl.ds(a * SIDE * LANE, SIDE * LANE), :])
    high, rest = split(head)
    kept = jnp.where(lane < 2 * TAGS, high.astype(F32), rest.astype(F32))
    mp[...] = jnp.where(lane < 3 * TAGS, kept, F32(0.0)).astype(BF)

    for g in range(2, SIDE):
        give_back(g, groups[g])
    for copy in back:
        copy.wait_recv()

    token_side = cmat[...].T
    c_high, c_rest = split(token_side)
    logits = jnp.zeros((TOK, LANE), F32)
    for b in range(SIDE):
        r = ret[b]
        mix = nn(c_high, r) + nn(c_rest, r)
        for j in range(2):
            cols = pl.ds((SIDE * j + b) * LANE, LANE)
            base = tok_ref[:, pl.ds(pl.multiple_of(c * HALF + (SIDE * j + b) * LANE, LANE), LANE)]
            out = (base.astype(F32) + mix[:, j * LANE : (j + 1) * LANE]).astype(BF)
            layer_ref[:, cols] = out
            head_rows = tag4[pl.ds(pl.multiple_of(c * HALF + (SIDE * j + b) * LANE, LANE), LANE), :]
            logits = logits + nn(out, head_rows)
    lgs[...] = logits
    swap = send(lgs, lgr, dev(dc=1))
    swap.wait_recv()
    logits = lgs[...] + lgr[...]
    grown = jnp.exp(logits)
    total = jnp.sum(jnp.where(lane < TAGS, grown, F32(0.0)), axis=1, keepdims=True)
    hot = lax.rem(lane, TAGS) == labels_ref[...]
    grad = grown / total - jnp.where(hot, F32(1.0), F32(0.0))
    grad = jnp.where(lane < 3 * TAGS, grad, F32(0.0))
    slot = lax.dot_general(
        cmat[...], grad, (((1,), (0,)), ((), ())), preferred_element_type=F32, precision=EXACT
    )
    high, rest = split(slot)
    middle = (lane >= TAGS) & (lane < 2 * TAGS)
    gs[...] = jnp.where(middle, rest.astype(F32), high.astype(F32)).astype(BF).reshape(SIDE, CAP, LANE)

    spot_z = pl.ds(pl.multiple_of(y * BLOCK + z * CAP, 32), CAP)
    grads_z = [send(gs.at[at(z, d)], gx.at[spot_z], dev(dz=d)) for d in range(1, SIDE)]
    gx[spot_z, :] = gs[z]
    for copy in grads_z:
        copy.wait_recv()
    block = gx.at[rows_of(y)]
    grads_y = [send(block, block, dev(dy=d)) for d in range(1, SIDE)]

    ingp[...] = jnp.zeros_like(ingp)
    oacc[...] = jnp.zeros_like(oacc)

    for d in (0, 1, 3, 2):
        if d:
            grads_y[d - 1].wait_recv()
        rows = rows_of(at(y, -d))
        grad_up = (nt(gx[rows, :], mp[...]) * act[rows, :]).astype(BF)
        oacc[...] += 2.0 * tn(low[rows, :], grad_up)
        low_grad = (2.0 * nt(grad_up, aout)).astype(BF)
        for h in range(2):
            ingp[h] += tn(low_grad, xs[h, rows, :])

    swap = send(ingp.at[1 - c], fp, dev(dc=1))
    ox[x] = oacc[...].astype(BF)
    outs_x = [send(ox.at[x], ox.at[x], dev(dx=d)) for d in range(1, SIDE)]
    swap.wait_recv()
    fx[x] = (ingp[c] + fp[...]).astype(BF)
    ins_x = [send(fx.at[x], fx.at[x], dev(dx=d)) for d in range(1, SIDE)]
    for copy in outs_x:
        copy.wait_recv()
    oy[y] = four(ox).astype(BF)
    outs_y = [send(oy.at[y], oy.at[y], dev(dy=d)) for d in range(1, SIDE)]
    for copy in ins_x:
        copy.wait_recv()
    fy[y] = four(fx).astype(BF)
    ins_y = [send(fy.at[y], fy.at[y], dev(dy=d)) for d in range(1, SIDE)]
    for copy in outs_y:
        copy.wait_recv()
    for a in range(SIDE):
        outg_ref[:, pl.ds(a * FQ, FQ)] = oy[a].astype(F32)
    for copy in ins_y:
        copy.wait_recv()
    done[c] = four(fy)
    swap = send(done.at[c], done.at[c], dev(dc=1))
    swap.wait_recv()
    ing_ref[:, :HALF] = done[0]
    ing_ref[:, HALF:] = done[1]
    for copy in sent:
        copy.wait_send()


def local(tokens, expert_ids, gate_values, tag_labels, w_gate, w_up, w_down, adapter_in, adapter_out, tag_weight):
    vmem = pl.BlockSpec(memory_space=pltpu.VMEM)
    hbm = pl.BlockSpec(memory_space=pl.ANY)
    layer, in_grad, out_grad = pl.pallas_call(
        kernel,
        out_shape=(
            jax.ShapeDtypeStruct((TOK, HALF), BF),
            jax.ShapeDtypeStruct((RANK, DIM), F32),
            jax.ShapeDtypeStruct((RANK, SHARD), F32),
        ),
        in_specs=[vmem] * 7 + [hbm] * 3,
        out_specs=(vmem, vmem, vmem),
        scratch_shapes=[
            pltpu.VMEM((SIDE, SIDE, LANE, FQ), BF),
            pltpu.VMEM((SIDE, SIDE, LANE, FQ), BF),
            pltpu.VMEM((SIDE, SIDE, FQ, LANE), BF),
            pltpu.VMEM((SIDE, CAP, HALF), BF),
            pltpu.VMEM((2, ROWS, HALF), BF),
            pltpu.VMEM((ROWS, FQ), F32),
            pltpu.VMEM((ROWS, FQ), BF),
            pltpu.VMEM((ROWS, RANK), BF),
            pltpu.VMEM((BLOCK, TOK), BF),
            pltpu.VMEM((BLOCK, TOK), F32),
            pltpu.VMEM((SIDE, ROWS, 2 * LANE), F32),
            pltpu.VMEM((SIDE, ROWS, 2 * LANE), BF),
            pltpu.VMEM((SIDE, ROWS, 2 * LANE), BF),
            pltpu.VMEM((SIDE, ROWS, 2 * LANE), BF),
            pltpu.VMEM((SIDE - 1, SIDE, BLOCK, 2 * LANE), BF),
            pltpu.VMEM((SIDE, SIDE, CAP, 2 * LANE), BF),
            pltpu.VMEM((SIDE, BLOCK, 2 * LANE), BF),
            pltpu.VMEM((TOK, LANE), F32),
            pltpu.VMEM((TOK, LANE), F32),
            pltpu.VMEM((DIM, LANE), BF),
            pltpu.VMEM((FQ, LANE), BF),
            pltpu.VMEM((SIDE, CAP, LANE), BF),
            pltpu.VMEM((ROWS, LANE), BF),
            pltpu.VMEM((2, RANK, HALF), F32),
            pltpu.VMEM((RANK, HALF), F32),
            pltpu.VMEM((SIDE, RANK, HALF), BF),
            pltpu.VMEM((SIDE, RANK, FQ), BF),
            pltpu.VMEM((SIDE, RANK, HALF), BF),
            pltpu.VMEM((SIDE, RANK, FQ), BF),
            pltpu.VMEM((2, RANK, HALF), F32),
            pltpu.VMEM((RANK, FQ), F32),
            pltpu.SemaphoreType.DMA((320,)),
        ],
        compiler_params=pltpu.CompilerParams(
            collective_id=0, has_side_effects=True, vmem_limit_bytes=62 * 1024 * 1024
        ),
    )(
        expert_ids.T, gate_values.T, tag_labels.reshape(TOK, 1), tokens,
        adapter_in[0], adapter_out[0], tag_weight, w_gate, w_up, w_down,
    )
    return layer, in_grad[None], out_grad[None]


def solution(mesh):
    in_specs = (
        P(("dp", "expert"), None),
        P(("dp", "expert"), None),
        P(("dp", "expert"), None),
        P(("dp", "expert")),
        P("expert", "dp", "tensor"),
        P("expert", "dp", "tensor"),
        P("expert", "tensor", "dp"),
        P("expert", None, None),
        P("expert", None, "tensor"),
        P(),
    )
    out_specs = (
        P(("dp", "expert"), "tensor"),
        P("expert", None, None),
        P("expert", None, "tensor"),
    )
    return jax.shard_map(local, mesh=mesh, in_specs=in_specs, out_specs=out_specs, check_vma=False)
```
